32 devices in a mesh: rows: 8 (over z, x), modes: 4 (over y, core).
Axes of the slice: x: 2, y: 2, z: 4, core: 2. Of those that a mesh axis runs over, the one named last changes fastest.
Arguments:
- test_basis: bfloat16 [4096, 5, 256], P('rows'), may hold values from -0.0390625 to 0.0390625
- deim_basis: bfloat16 [4096, 5, 512], P('rows', None, 'modes'), may hold values from -6 to 6
- trial_basis: bfloat16 [4096, 5, 256], P('rows'), may hold values from -6 to 6
- jacobian: float32 [2048, 7, 5], P('rows'), may hold values from -1 to 1
- neighbours: int32 [2048, 7], P('rows'), may hold values from 0 to 4095, as said below
- counts: int32 [8], P('rows'), may hold values from 1 to 256, 512 in all
- sample_inverse: float32 [512, 512], P('modes'), may hold values from -0.01171875 to 0.01171875
Outputs:
- reduced_operator: float32 [256, 256], P('modes', 'rows')
The draws below stay inside these ranges and needn't reach their ends.
Inputs may be any that keep to these rules, and one draw needn't show every extreme that they name: `neighbours`: the first entry of row g is the sampled cell, which lies among the 512 cells of device g // 256; every other entry lies within 128 cells of it. Device r uses its first counts[r] slots; the counts sum to 512.
All inputs are finite; a program needn't handle non-finite values.
Results may differ from the reference program's by a relative error of at most 0.0003.
Values may be sent and summed in bfloat16 or wider, within the bound.
A program may use at most 64 MiB of HBM per device.

```python
import math
import jax
import jax.numpy as jnp
import numpy as np
from jax import lax

K = 256
M = 512
NC = 5
NB = 7
HALO = 128
CELLS_DEV = 512
SLOT = 256
NCELLS = 4096
SAMPLES = 2048
N_ROWS = 8


def draw_neighbours(key, part):
    first, second = jax.random.split(jax.random.fold_in(key, 11))
    total = N_ROWS * SLOT
    device = jnp.arange(total, dtype=jnp.int32) // SLOT
    centre = device * CELLS_DEV + jax.random.randint(first, (total,), 0, CELLS_DEV)
    reach = jax.random.randint(second, (total, NB - 1), -HALO, HALO + 1)
    others = jnp.clip(centre[:, None] + reach, 0, N_ROWS * CELLS_DEV - 1)
    return jnp.concatenate([centre[:, None], others], axis=1).astype(jnp.int32)


def levels(stream_key, shape, shards, low, top_value):
    def one(dim, shards_of):
        draws = jax.random.uniform(jax.random.fold_in(jax.random.fold_in(stream_key, 6), dim), (shards_of,), jnp.float32, low / len(shards), top_value / len(shards))
        return jnp.repeat(jnp.exp(draws), shape[dim] // shards_of).reshape((-1,) + (1,) * (len(shape) - dim - 1))

    gain = one(*shards[0])
    for cut in shards[1:]:
        gain = gain * one(*cut)
    return gain


def split_up(count, total, bound, slope):
    loads = [(1 << 20) // math.isqrt(grade ** slope) + 1 for grade in range(2, count + 1)]
    surplus, given = total - bound - (count - 1), [1] * (count - 1)
    while surplus > 0:
        candidates = [i for i in range(count - 1) if given[i] < bound]
        pool, budget = sum([loads[i] for i in candidates]), surplus
        for i in candidates:
            more = min(bound - given[i], max(1, budget * loads[i] // pool), surplus)
            given[i] = given[i] + more
            surplus = surplus - more
    return np.array([bound] + given)


def uneven(own_key, amount, total, most, lean):
    if amount == 2:
        one = jax.random.randint(own_key, (), max(1, total - most), min(most, total - 1) + 1)
        return jnp.stack([one, total - one])
    tallies = jnp.asarray(split_up(amount, total, most, lean), jnp.int32)
    pairs = (amount - 1) // 2
    donor, receiver = tallies[1:1 + 2 * pairs:2], tallies[2:2 + 2 * pairs:2]
    room = jnp.minimum(donor - 1, most - receiver)
    moved = jax.random.randint(jax.random.fold_in(own_key, 1), (pairs,), 0, 1 << 20) % (room + 1)
    tallies = tallies.at[1:1 + 2 * pairs:2].set(donor - moved).at[2:2 + 2 * pairs:2].set(receiver + moved)
    return tallies[jax.random.permutation(jax.random.fold_in(own_key, 2), amount)]


def gaussian(rng, dims, width, most, cuts=(), held_as=jnp.bfloat16):
    drawn = jax.random.normal(rng, dims, jnp.float32) * width
    if len(cuts) > 0:
        drawn = levels(rng, dims, cuts, -0.22, 0.18) * drawn
    return jnp.clip(drawn, min=-most, max=most).astype(held_as)


def setup_inputs(seed: int = 0) -> dict:
    seeds = jax.random.split(jax.random.key(seed), 8)
    return {
        "test_basis": gaussian(seeds[0], (NCELLS, NC, K), (NCELLS * 5) ** -0.5, 0.0390625, ((0, 8),)),
        "deim_basis": gaussian(seeds[1], (NCELLS, NC, M), 1.0, 6.0, ((0, 8), (2, 4))),
        "trial_basis": gaussian(seeds[2], (NCELLS, NC, K), 1.0, 6.0, ((0, 8),)),
        "jacobian": gaussian(seeds[3], (SAMPLES, NB, NC), (NB * 5) ** -0.5, 1.0, ((0, 8),), jnp.float32),
        "neighbours": draw_neighbours(jax.random.fold_in(seeds[7], 71), 0),
        "counts": uneven(seeds[5], N_ROWS, M, SLOT, 2).astype(jnp.int32),
        "sample_inverse": gaussian(seeds[6], (M, M), (M * M) ** -0.5, 0.01171875, ((0, 4),), jnp.float32),
    }


def reference(test_basis, deim_basis, trial_basis, jacobian, neighbours, counts, sample_inverse):
    flat_test = test_basis.reshape(-1, K).astype(jnp.float32)
    flat_deim = deim_basis.reshape(-1, M).astype(jnp.float32)
    projection = lax.dot_general(flat_test, flat_deim, (((0,), (0,)), ((), ())), precision=lax.Precision.HIGHEST, preferred_element_type=jnp.float32)
    offset = jnp.cumsum(counts) - counts
    total = neighbours.shape[0]
    slot_ids = jnp.arange(total, dtype=jnp.int32)
    device = slot_ids // SLOT
    within = slot_ids % SLOT
    live = within < counts[device]
    row_ids = jnp.where(live, offset[device] + within, 0).astype(jnp.int32)
    picked = trial_basis[neighbours].astype(jnp.float32)
    contrib = jnp.einsum("snj,snjk->sk", jacobian.astype(jnp.float32), picked, precision=lax.Precision.HIGHEST)
    contrib = contrib * live[:, None].astype(jnp.float32)
    sampled = jnp.zeros((M, K), jnp.float32).at[row_ids].add(contrib)
    folded = jnp.dot(projection, sample_inverse, precision=lax.Precision.HIGHEST, preferred_element_type=jnp.float32)
    return jnp.dot(folded, sampled, precision=lax.Precision.HIGHEST, preferred_element_type=jnp.float32)
```

```python
import functools

import jax
import jax.numpy as jnp
from jax import lax
from jax.experimental import pallas as pl
from jax.experimental.pallas import tpu as pltpu
from jax.sharding import PartitionSpec as P

HALO = 128
MESH = pl.DeviceIdType.MESH
CHUNK = 32


def round_up(x, m):
    return (x + m - 1) // m * m


def nt(a, b):
    return lax.dot_general(
        a, b, (((1,), (1,)), ((), ())),
        precision=lax.Precision.HIGHEST, preferred_element_type=jnp.float32,
    )


def tn(a, b):
    return lax.dot_general(
        a, b, (((0,), (0,)), ((), ())), preferred_element_type=jnp.float32
    )


def kernel(groups, parts, comps,
           test_hbm, deim_hbm, trial_hbm, jac_hbm, nbr_hbm, counts_ref, inv_hbm,
           out_ref,
           test, deim, trial, inv, jac, nbr, cnt, packed, sparse,
           g_own, g_in, p_all, s_own, s_in, s_all, o_own, o_in,
           load_sem, jac_send, jac_recv, nbr_send, nbr_recv, cnt_send, cnt_recv,
           g_send, g_recv, p_send, p_recv, s_send, s_recv, t_send, t_recv, o_send, o_recv):
    r = lax.axis_index("rows")
    m = lax.axis_index("modes")
    cells = test.shape[0] // comps
    coupled, slots = nbr.shape[1], nbr.shape[2]
    modes = deim.shape[1]
    cols = g_in.shape[1]
    rows_out = o_own.shape[2]
    pad = round_up(coupled, 8)

    def peer(t):
        return lax.rem(r + t, groups)

    def mate(t):
        return lax.rem(m + t, parts)

    loads = []
    for j in range(comps):
        at = pl.ds(j * cells, cells)
        for i, (src, dst) in enumerate(((test_hbm, test), (deim_hbm, deim), (trial_hbm, trial))):
            loads.append(pltpu.make_async_copy(src.at[at], dst.at[at], load_sem.at[i, j]))
    own_jac = pltpu.make_async_copy(jac_hbm, jac.at[1], load_sem.at[3, 0])
    own_nbr = pltpu.make_async_copy(nbr_hbm, nbr.at[1], load_sem.at[3, 1])
    own_inv = pltpu.make_async_copy(inv_hbm, inv, load_sem.at[3, 2])
    own_jac.start()
    own_nbr.start()
    for j in range(comps):
        loads[3 * j].start()
        loads[3 * j + 1].start()
    for j in range(comps):
        loads[3 * j + 2].start()
    own_inv.start()

    cnt[pl.ds(r, 1)] = jnp.full((1,) + cnt.shape[1:], counts_ref[0], jnp.int32)
    packed[...] = jnp.zeros_like(packed)

    barrier = pltpu.get_barrier_semaphore()
    for t in range(1, groups):
        pl.semaphore_signal(barrier, inc=1, device_id={"rows": peer(t)}, device_id_type=MESH)
    for t in range(1, parts):
        pl.semaphore_signal(barrier, inc=1, device_id={"modes": mate(t)}, device_id_type=MESH)
    pl.semaphore_wait(barrier, groups + parts - 2)

    sent = []
    small = []
    for i, t in ((0, 1), (1, groups - 1)):
        slot = 2 * i
        for src, dst, ss, rs in ((jac_hbm, jac, jac_send, jac_recv), (nbr_hbm, nbr, nbr_send, nbr_recv)):
            small.append(pltpu.make_async_remote_copy(
                src, dst.at[slot], ss.at[i], rs.at[i],
                device_id={"rows": peer(t)}, device_id_type=MESH))
    for t in range(1, groups):
        small.append(pltpu.make_async_remote_copy(
            cnt.at[r], cnt.at[r], cnt_send.at[t], cnt_recv.at[t],
            device_id={"rows": peer(t)}, device_id_type=MESH))
    for c in small:
        c.start()

    g = jnp.zeros(g_own.shape, jnp.float32)
    for j in range(comps):
        loads[3 * j].wait()
        loads[3 * j + 1].wait()
        at = pl.ds(j * cells, cells)
        g += tn(test[at], deim[at])
    g_own[...] = g
    g_copies = []
    for t in range(1, groups):
        g_copies.append(pltpu.make_async_remote_copy(
            g_own.at[pl.ds(pl.multiple_of(peer(t) * cols, 8), cols)], g_in.at[r],
            g_send.at[t], g_recv.at[t],
            device_id={"rows": peer(t)}, device_id_type=MESH))
    for c in g_copies:
        c.start()

    own_jac.wait()
    own_nbr.wait()
    for c in small:
        c.wait()
    for i in range(3):
        for j in range(comps):
            packed[j * pad:j * pad + coupled, i * slots:(i + 1) * slots] = jac[i, j]
        packed[comps * pad:comps * pad + coupled, i * slots:(i + 1) * slots] = nbr[i].astype(jnp.float32)
    q_ids = lax.broadcasted_iota(jnp.int32, (slots, modes), 1) + m * modes
    s_ids = lax.broadcasted_iota(jnp.int32, (slots, modes), 0)
    picks = []
    for i in range(3):
        d = lax.rem(r + i + groups - 1, groups)
        offset = jnp.zeros((1, modes), jnp.int32)
        for e in range(groups):
            offset += jnp.where(e < d, cnt[e, 0:1], 0)
        held = cnt[d, 0:1]
        hit = (q_ids - offset == s_ids) & (s_ids < held)
        picks.append(jnp.where(hit, 1.0, 0.0).astype(jnp.bfloat16))
    pick = jnp.concatenate(picks, axis=0)
    x = packed[...]
    hi = x.astype(jnp.bfloat16)
    rest = x - hi.astype(jnp.float32)
    mid = rest.astype(jnp.bfloat16)
    lo = (rest - mid.astype(jnp.float32)).astype(jnp.bfloat16)
    split = jnp.concatenate([hi, mid, lo], axis=0)
    got = lax.dot_general(split, pick, (((1,), (0,)), ((), ())), preferred_element_type=jnp.float32)
    n = x.shape[0]
    got = got[:n] + got[n:2 * n] + got[2 * n:]

    near = [got[comps * pad + k:comps * pad + k + 1] - (r * cells).astype(jnp.float32) for k in range(coupled)]
    entry = [[got[j * pad + k:j * pad + k + 1] for k in range(coupled)] for j in range(comps)]
    base = lax.broadcasted_iota(jnp.int32, (CHUNK, modes), 0).astype(jnp.float32)

    def build(step, carry):
        here = base + (step * CHUNK).astype(jnp.float32)
        acc = [jnp.zeros((CHUNK, modes), jnp.float32) for _ in range(comps)]
        for k in range(coupled):
            hit = here == near[k]
            for j in range(comps):
                acc[j] += jnp.where(hit, entry[j][k], 0.0)
        for j in range(comps):
            hi = acc[j].astype(jnp.bfloat16)
            lo = (acc[j] - hi.astype(jnp.float32)).astype(jnp.bfloat16)
            at = pl.ds(pl.multiple_of(j * cells + step * CHUNK, CHUNK), CHUNK)
            sparse[at, :modes] = hi
            sparse[at, modes:] = lo
        return carry

    lax.fori_loop(0, cells // CHUNK, build, 0)

    s = jnp.zeros((trial.shape[1], 2 * modes), jnp.float32)
    for j in range(comps):
        loads[3 * j + 2].wait()
        at = pl.ds(j * cells, cells)
        s += tn(trial[at], sparse[at])
    s_own[...] = s[:, :modes] + s[:, modes:]
    s_copies = []
    for t in range(1, groups):
        s_copies.append(pltpu.make_async_remote_copy(
            s_own.at[pl.ds(pl.multiple_of(peer(t) * cols, 8), cols)], s_in.at[r],
            s_send.at[t], s_recv.at[t],
            device_id={"rows": peer(t)}, device_id_type=MESH))
    for c in s_copies:
        c.start()

    mine = pl.ds(pl.multiple_of(r * cols, 8), cols)
    total = g_own[mine]
    for t in range(1, groups):
        g_copies[t - 1].wait_recv()
        total += g_in[lax.rem(r - t + groups, groups)]
    p_all[mine] = total
    p_copies = []
    for t in range(1, groups):
        p_copies.append(pltpu.make_async_remote_copy(
            p_all.at[mine], p_all.at[mine], p_send.at[t], p_recv.at[t],
            device_id={"rows": peer(t)}, device_id_type=MESH))
    for c in p_copies:
        c.start()

    total = s_own[mine]
    for t in range(1, groups):
        s_copies[t - 1].wait_recv()
        total += s_in[lax.rem(r - t + groups, groups)]
    s_all[m] = total
    t_copies = []
    for t in range(1, parts):
        t_copies.append(pltpu.make_async_remote_copy(
            s_all.at[m], s_all.at[m], t_send.at[t], t_recv.at[t],
            device_id={"modes": mate(t)}, device_id_type=MESH))
    for c in t_copies:
        c.start()
    own_inv.wait()
    for c in t_copies:
        c.wait()
    folded = jnp.zeros((cols, modes), jnp.float32)
    for e in range(parts):
        folded += nt(s_all[e], inv[:, e * modes:(e + 1) * modes])
    for c in p_copies:
        c.wait()
    for e in range(parts):
        o_own[e] = nt(folded, p_all[e * rows_out:(e + 1) * rows_out])
    o_copies = []
    for t in range(1, parts):
        o_copies.append(pltpu.make_async_remote_copy(
            o_own.at[mate(t)], o_in.at[m], o_send.at[t], o_recv.at[t],
            device_id={"modes": mate(t)}, device_id_type=MESH))
    for c in o_copies:
        c.start()
    for c in g_copies + s_copies:
        c.wait_send()
    total = o_own[m]
    for t in range(1, parts):
        o_copies[t - 1].wait()
        total += o_in[lax.rem(m - t + parts, parts)]
    out_ref[...] = total


def fused(groups, parts, test_basis, deim_basis, trial_basis, jacobian, neighbours, counts, sample_inverse):
    cells, comps, width = trial_basis.shape
    slots, coupled = neighbours.shape
    modes, total_modes = sample_inverse.shape
    cols = width // groups
    rows_out = width // parts
    flat = lambda b: b.transpose(1, 0, 2).reshape(cells * comps, b.shape[2])
    f32, bf16, i32 = jnp.float32, jnp.bfloat16, jnp.int32
    dma = lambda *shape: pltpu.SemaphoreType.DMA(shape)
    any_spec = pl.BlockSpec(memory_space=pl.ANY)
    out = pl.pallas_call(
        functools.partial(kernel, groups, parts, comps),
        out_shape=jax.ShapeDtypeStruct((cols, rows_out), f32),
        in_specs=[any_spec] * 5 + [pl.BlockSpec(memory_space=pltpu.SMEM), any_spec],
        out_specs=pl.BlockSpec(memory_space=pltpu.VMEM),
        scratch_shapes=[
            pltpu.VMEM((cells * comps, width), bf16),
            pltpu.VMEM((cells * comps, modes), bf16),
            pltpu.VMEM((cells * comps, width), bf16),
            pltpu.VMEM((modes, total_modes), f32),
            pltpu.VMEM((3, comps, coupled, slots), f32),
            pltpu.VMEM((3, coupled, slots), i32),
            pltpu.VMEM((groups, 8, modes), i32),
            pltpu.VMEM(((comps + 1) * round_up(coupled, 8), 3 * slots), f32),
            pltpu.VMEM((cells * comps, 2 * modes), bf16),
            pltpu.VMEM((width, modes), f32),
            pltpu.VMEM((groups, cols, modes), f32),
            pltpu.VMEM((width, modes), f32),
            pltpu.VMEM((width, modes), f32),
            pltpu.VMEM((groups, cols, modes), f32),
            pltpu.VMEM((parts, cols, modes), f32),
            pltpu.VMEM((parts, cols, rows_out), f32),
            pltpu.VMEM((parts, cols, rows_out), f32),
            dma(4, max(comps, 3)), dma(2), dma(2), dma(2), dma(2),
            dma(groups), dma(groups),
            dma(groups), dma(groups), dma(groups), dma(groups),
            dma(groups), dma(groups), dma(parts), dma(parts), dma(parts), dma(parts),
        ],
        compiler_params=pltpu.CompilerParams(collective_id=0, has_side_effects=True),
        name="reduced",
    )(flat(test_basis), flat(deim_basis), flat(trial_basis), jacobian.transpose(2, 1, 0),
      neighbours.T, counts, sample_inverse)
    return out.T


def entering(part, axis, combine, identity):
    place = lax.axis_index(axis)
    gathered = lax.all_gather(part, axis)
    state = jnp.zeros_like(part) + jnp.asarray(identity, part.dtype)

    def one(turn, state):
        return combine(state, lax.dynamic_index_in_dim(gathered, turn, 0, False))

    return lax.fori_loop(0, place, one, state)


def extended(block, sides, width):
    for axis, dim in sides:
        count = lax.axis_size(axis)
        forward = [(i, i + 1) for i in range(count - 1)]
        backward = [(target, source) for source, target in forward]
        low = lax.ppermute(
            lax.slice_in_dim(block, block.shape[dim] - width, None, axis=dim), axis, forward
        )
        high = lax.ppermute(lax.slice_in_dim(block, 0, width, axis=dim), axis, backward)
        block = jnp.concatenate([low, block, high], axis=dim)
    return block


def add_ints(earlier, later):
    return earlier + later


def plain(test_basis, deim_basis, trial_basis, jacobian, neighbours, counts, sample_inverse):
    cells, comps, width = trial_basis.shape
    slots, coupled = neighbours.shape
    total_modes = sample_inverse.shape[1]
    rank = lax.axis_index("rows")
    groups = lax.axis_size("rows")
    flat_test = test_basis.reshape(cells * comps, width)
    flat_deim = deim_basis.reshape(cells * comps, deim_basis.shape[2])
    partial_g = lax.dot_general(
        flat_test, flat_deim, (((0,), (0,)), ((), ())), preferred_element_type=jnp.float32
    )
    offset = entering(counts, "rows", add_ints, jnp.zeros((1,), jnp.int32))
    slot_ids = jnp.arange(slots, dtype=jnp.int32)
    live = slot_ids < counts[0]
    row_ids = jnp.where(live, offset[0] + slot_ids, -1)
    first_cell = rank * cells
    widened = extended(trial_basis, (("rows", 0),), HALO)
    local = neighbours - (first_cell - HALO)
    picked = widened[local].astype(jnp.float32)
    contrib = jnp.einsum("snj,snjk->sk", jacobian, picked, precision=lax.Precision.HIGHEST)
    mode_ids = jnp.arange(total_modes, dtype=jnp.int32)[None, :]
    total_g = lax.psum(partial_g, "rows")
    folded = jnp.dot(
        total_g, sample_inverse, precision=lax.Precision.HIGHEST, preferred_element_type=jnp.float32
    )
    row_tags = jnp.broadcast_to(row_ids[:, None].astype(jnp.float32), (row_ids.shape[0], groups))
    arrived, arrived_tags = (
        lax.all_to_all(contrib, "rows", split_axis=1, concat_axis=0, tiled=True),
        lax.all_to_all(row_tags, "rows", split_axis=1, concat_axis=0, tiled=True),
    )
    received_ids = arrived_tags[:, 0].astype(jnp.int32)
    selector = (received_ids[:, None] == mode_ids).astype(jnp.float32)
    column_b = lax.dot_general(
        selector,
        arrived,
        (((0,), (0,)), ((), ())),
        precision=lax.Precision.HIGHEST,
        preferred_element_type=jnp.float32,
    )
    column_share = jnp.dot(
        folded, column_b, precision=lax.Precision.HIGHEST, preferred_element_type=jnp.float32
    )
    return lax.psum_scatter(column_share, "modes", scatter_dimension=0, tiled=True)


def solution(mesh):
    groups, parts = mesh.shape["rows"], mesh.shape["modes"]

    def shards(*args):
        cells, comps, width = args[2].shape
        modes = args[6].shape[0]
        slots = args[4].shape[0]
        tiled = (
            groups >= 3 and parts >= 2 and cells >= HALO
            and width % (8 * groups) == 0 and width % (8 * parts) == 0
            and modes % 128 == 0 and slots % 128 == 0 and cells % CHUNK == 0
        )
        return fused(groups, parts, *args) if tiled else plain(*args)

    in_specs = (
        P("rows", None, None),
        P("rows", None, "modes"),
        P("rows", None, None),
        P("rows", None, None),
        P("rows", None),
        P("rows"),
        P("modes", None),
    )
    out_specs = P("modes", "rows")
    return jax.shard_map(shards, mesh=mesh, in_specs=in_specs, out_specs=out_specs, check_vma=False)
```

```python
import functools

import jax
import jax.numpy as jnp
from jax import lax
from jax.experimental import pallas as pl
from jax.experimental.pallas import tpu as pltpu
from jax.sharding import PartitionSpec as P

HALO = 128
MESH = pl.DeviceIdType.MESH
CHUNK = 32


def round_up(x, m):
    return (x + m - 1) // m * m


def pieces(x):
    hi = x.astype(jnp.bfloat16)
    return hi, (x - hi.astype(jnp.float32)).astype(jnp.bfloat16)


def nt_split(a, b):
    rows = a[0].shape[0]
    contract = (((1,), (1,)), ((), ()))
    main = lax.dot_general(jnp.concatenate(a, axis=0), b[0], contract, preferred_element_type=jnp.float32)
    rest = lax.dot_general(a[0], b[1], contract, preferred_element_type=jnp.float32)
    return main[:rows] + (main[rows:] + rest)


def tn(a, b):
    return lax.dot_general(
        a, b, (((0,), (0,)), ((), ())), preferred_element_type=jnp.float32
    )


def kernel(groups, parts, comps, coupled,
           test_hbm, deim_hbm, trial_hbm, jac_hbm, nbr_hbm, counts_ref, inv_hbm,
           out_ref,
           test, deim, trial, inv, jac, nbr, cnt, slot_data, turned, sparse,
           g_own, g_in, p_all, p_hi, p_lo, s_own, s_in, s_all, inv_hi, inv_lo, o_own, o_in,
           load_sem, slot_send, slot_recv, cnt_send, cnt_recv,
           g_send, g_recv, p_send, p_recv, s_send, s_recv, t_send, t_recv, o_send, o_recv):
    r = lax.axis_index("rows")
    m = lax.axis_index("modes")
    cells = test.shape[0] // comps
    slots = nbr.shape[1]
    modes = deim.shape[1]
    cols = g_in.shape[1]
    rows_out = o_own.shape[2]
    pad = round_up(coupled, 8)
    far_first = sorted(range(1, groups), key=lambda t: -min(t, groups - t))

    def peer(t):
        return lax.rem(r + t, groups)

    def mate(t):
        return lax.rem(m + t, parts)

    def to_peer(src, dst, send, recv, t):
        return pltpu.make_async_remote_copy(
            src, dst, send.at[t], recv.at[t], device_id={"rows": peer(t)}, device_id_type=MESH)

    def to_mate(src, dst, send, recv, t):
        return pltpu.make_async_remote_copy(
            src, dst, send.at[t], recv.at[t], device_id={"modes": mate(t)}, device_id_type=MESH)

    def block(t):
        return pl.ds(pl.multiple_of(peer(t) * cols, 8), cols)

    mine = pl.ds(pl.multiple_of(r * cols, 8), cols)

    barrier = pltpu.get_barrier_semaphore()
    for t in far_first:
        pl.semaphore_signal(barrier, inc=1, device_id={"rows": peer(t)}, device_id_type=MESH)
    for t in range(1, parts):
        pl.semaphore_signal(barrier, inc=1, device_id={"modes": mate(t)}, device_id_type=MESH)

    loads = []
    for j in range(comps):
        at = pl.ds(j * cells, cells)
        for i, (src, dst) in enumerate(((test_hbm, test), (deim_hbm, deim), (trial_hbm, trial))):
            loads.append(pltpu.make_async_copy(src.at[at], dst.at[at], load_sem.at[i, j]))
    own_jac = pltpu.make_async_copy(jac_hbm, jac, load_sem.at[3, 0])
    own_nbr = pltpu.make_async_copy(nbr_hbm, nbr, load_sem.at[3, 1])
    own_inv = pltpu.make_async_copy(inv_hbm, inv, load_sem.at[3, 2])
    own_jac.start()
    own_nbr.start()
    for j in range(comps):
        loads[3 * j].start()
        loads[3 * j + 1].start()
    for j in range(comps):
        loads[3 * j + 2].start()
    own_inv.start()

    cnt[pl.ds(r, 1)] = jnp.full((1,) + cnt.shape[1:], counts_ref[0], jnp.int32)
    own_jac.wait()
    own_nbr.wait()
    slot_data[1] = jnp.zeros(slot_data.shape[1:], jnp.float32)
    for j in range(comps):
        slot_data[1, j * pad:j * pad + coupled] = jac[j]
    slot_data[1, comps * pad:comps * pad + coupled] = nbr[...].astype(jnp.float32)
    g = jnp.zeros(g_own.shape, jnp.float32)
    for j in range(comps):
        loads[3 * j].wait()
        loads[3 * j + 1].wait()
        at = pl.ds(j * cells, cells)
        g += tn(test[at], deim[at])
    g_own[...] = g

    pl.semaphore_wait(barrier, groups + parts - 2)

    small = []
    for i, t in ((0, 1), (1, groups - 1)):
        small.append(pltpu.make_async_remote_copy(
            slot_data.at[1], slot_data.at[2 * i],
            slot_send.at[i], slot_recv.at[i],
            device_id={"rows": peer(t)}, device_id_type=MESH))
    small += [to_peer(cnt.at[r], cnt.at[r], cnt_send, cnt_recv, t) for t in far_first]
    for c in small:
        c.start()
    g_copies = [to_peer(g_own.at[block(t)], g_in.at[r], g_send, g_recv, t) for t in far_first]
    for c in g_copies:
        c.start()

    for j in range(comps):
        loads[3 * j + 2].wait()
        at = pl.ds(j * cells, cells)
        turned[:, at] = trial[at].T
    own_inv.wait()
    for e in range(parts):
        inv_hi[e], inv_lo[e] = pieces(inv[:, e * modes:(e + 1) * modes])

    for c in small:
        c.wait()
    q_ids = lax.broadcasted_iota(jnp.int32, (slots, modes), 1) + m * modes
    s_ids = lax.broadcasted_iota(jnp.int32, (slots, modes), 0)
    n = slot_data.shape[1]
    got = jnp.zeros((3 * n, modes), jnp.float32)
    for i in range(3):
        d = lax.rem(r + i + groups - 1, groups)
        offset = jnp.zeros((1, modes), jnp.int32)
        for e in range(groups):
            offset += jnp.where(e < d, cnt[e, 0:1], 0)
        hit = (q_ids - offset == s_ids) & (s_ids < cnt[d, 0:1])
        pick = jnp.where(hit, 1.0, 0.0).astype(jnp.bfloat16)
        x = slot_data[i]
        hi = x.astype(jnp.bfloat16)
        rest = x - hi.astype(jnp.float32)
        mid = rest.astype(jnp.bfloat16)
        lo = (rest - mid.astype(jnp.float32)).astype(jnp.bfloat16)
        split = jnp.concatenate([hi, mid, lo], axis=0)
        got += lax.dot_general(split, pick, (((1,), (0,)), ((), ())), preferred_element_type=jnp.float32)
    got = got[:n] + got[n:2 * n] + got[2 * n:]

    near = [got[comps * pad + k:comps * pad + k + 1] - (r * cells).astype(jnp.float32) for k in range(coupled)]
    entry = [[got[j * pad + k:j * pad + k + 1] for k in range(coupled)] for j in range(comps)]
    base = lax.broadcasted_iota(jnp.int32, (CHUNK, modes), 0).astype(jnp.float32)

    def build(step, carry):
        here = base + (step * CHUNK).astype(jnp.float32)
        acc = [jnp.zeros((CHUNK, modes), jnp.float32) for _ in range(comps)]
        for k in range(coupled):
            hit = here == near[k]
            for j in range(comps):
                acc[j] += jnp.where(hit, entry[j][k], 0.0)
        for j in range(comps):
            hi = acc[j].astype(jnp.bfloat16)
            lo = (acc[j] - hi.astype(jnp.float32)).astype(jnp.bfloat16)
            at = pl.ds(pl.multiple_of(j * cells + step * CHUNK, CHUNK), CHUNK)
            sparse[at, :modes] = hi
            sparse[at, modes:] = lo
        return carry

    lax.fori_loop(0, cells // CHUNK, build, 0)

    s = lax.dot_general(
        turned[...], sparse[...], (((1,), (0,)), ((), ())), preferred_element_type=jnp.float32)
    s_own[...] = s[:, :modes] + s[:, modes:]
    s_copies = [to_peer(s_own.at[block(t)], s_in.at[r], s_send, s_recv, t) for t in far_first]
    for c in s_copies:
        c.start()

    total = g_own[mine]
    for t, c in zip(far_first, g_copies):
        c.wait_recv()
        total += g_in[lax.rem(r - t + groups, groups)]
    p_all[mine] = total
    p_copies = [to_peer(p_all.at[mine], p_all.at[mine], p_send, p_recv, t) for t in far_first]
    for c in p_copies:
        c.start()

    total = s_own[mine]
    for t, c in zip(far_first, s_copies):
        c.wait_recv()
        total += s_in[lax.rem(r - t + groups, groups)]
    s_all[m] = total
    t_copies = [to_mate(s_all.at[m], s_all.at[m], t_send, t_recv, t) for t in range(1, parts)]
    for c in t_copies:
        c.start()
    folded = nt_split(pieces(total), (inv_hi[m], inv_lo[m]))
    for c in p_copies:
        c.wait()
    for e in range(parts):
        p_hi[e], p_lo[e] = pieces(p_all[e * rows_out:(e + 1) * rows_out])
    for t, c in zip(range(1, parts), t_copies):
        c.wait()
        e = lax.rem(m - t + parts, parts)
        folded += nt_split(pieces(s_all[e]), (inv_hi[e], inv_lo[e]))
    folded = pieces(folded)
    for e in range(parts):
        o_own[e] = nt_split(folded, (p_hi[e], p_lo[e]))
    o_copies = [to_mate(o_own.at[mate(t)], o_in.at[m], o_send, o_recv, t) for t in range(1, parts)]
    for c in o_copies:
        c.start()
    for c in g_copies + s_copies:
        c.wait_send()
    total = o_own[m]
    for t in range(1, parts):
        o_copies[t - 1].wait()
        total += o_in[lax.rem(m - t + parts, parts)]
    out_ref[...] = total


def fused(groups, parts, test_basis, deim_basis, trial_basis, jacobian, neighbours, counts, sample_inverse):
    cells, comps, width = trial_basis.shape
    slots, coupled = neighbours.shape
    modes, total_modes = sample_inverse.shape
    cols = width // groups
    rows_out = width // parts
    flat = lambda b: b.transpose(1, 0, 2).reshape(cells * comps, b.shape[2])
    f32, bf16, i32 = jnp.float32, jnp.bfloat16, jnp.int32
    dma = lambda *shape: pltpu.SemaphoreType.DMA(shape)
    any_spec = pl.BlockSpec(memory_space=pl.ANY)
    out = pl.pallas_call(
        functools.partial(kernel, groups, parts, comps, coupled),
        out_shape=jax.ShapeDtypeStruct((cols, rows_out), f32),
        in_specs=[any_spec] * 5 + [pl.BlockSpec(memory_space=pltpu.SMEM), any_spec],
        out_specs=pl.BlockSpec(memory_space=pltpu.VMEM),
        scratch_shapes=[
            pltpu.VMEM((cells * comps, width), bf16),
            pltpu.VMEM((cells * comps, modes), bf16),
            pltpu.VMEM((cells * comps, width), bf16),
            pltpu.VMEM((modes, total_modes), f32),
            pltpu.VMEM((comps, coupled, slots), f32),
            pltpu.VMEM((coupled, slots), i32),
            pltpu.VMEM((groups, 8, modes), i32),
            pltpu.VMEM((3, (comps + 1) * round_up(coupled, 8), slots), f32),
            pltpu.VMEM((width, cells * comps), bf16),
            pltpu.VMEM((cells * comps, 2 * modes), bf16),
            pltpu.VMEM((width, modes), f32),
            pltpu.VMEM((groups, cols, modes), f32),
            pltpu.VMEM((width, modes), f32),
            pltpu.VMEM((parts, rows_out, modes), bf16),
            pltpu.VMEM((parts, rows_out, modes), bf16),
            pltpu.VMEM((width, modes), f32),
            pltpu.VMEM((groups, cols, modes), f32),
            pltpu.VMEM((parts, cols, modes), f32),
            pltpu.VMEM((parts, modes, modes), bf16),
            pltpu.VMEM((parts, modes, modes), bf16),
            pltpu.VMEM((parts, cols, rows_out), f32),
            pltpu.VMEM((parts, cols, rows_out), f32),
            dma(4, max(comps, 3)), dma(2), dma(2), dma(groups), dma(groups),
            dma(groups), dma(groups), dma(groups), dma(groups),
            dma(groups), dma(groups), dma(parts), dma(parts), dma(parts), dma(parts),
        ],
        compiler_params=pltpu.CompilerParams(collective_id=0, has_side_effects=True),
        name="reduced",
    )(flat(test_basis), flat(deim_basis), flat(trial_basis), jacobian.transpose(2, 1, 0),
      neighbours.T, counts, sample_inverse)
    return out.T


def entering(part, axis, combine, identity):
    place = lax.axis_index(axis)
    gathered = lax.all_gather(part, axis)
    state = jnp.zeros_like(part) + jnp.asarray(identity, part.dtype)

    def one(turn, state):
        return combine(state, lax.dynamic_index_in_dim(gathered, turn, 0, False))

    return lax.fori_loop(0, place, one, state)


def extended(block, sides, width):
    for axis, dim in sides:
        count = lax.axis_size(axis)
        forward = [(i, i + 1) for i in range(count - 1)]
        backward = [(target, source) for source, target in forward]
        low = lax.ppermute(
            lax.slice_in_dim(block, block.shape[dim] - width, None, axis=dim), axis, forward
        )
        high = lax.ppermute(lax.slice_in_dim(block, 0, width, axis=dim), axis, backward)
        block = jnp.concatenate([low, block, high], axis=dim)
    return block


def add_ints(earlier, later):
    return earlier + later


def plain(test_basis, deim_basis, trial_basis, jacobian, neighbours, counts, sample_inverse):
    cells, comps, width = trial_basis.shape
    slots, coupled = neighbours.shape
    total_modes = sample_inverse.shape[1]
    rank = lax.axis_index("rows")
    groups = lax.axis_size("rows")
    flat_test = test_basis.reshape(cells * comps, width)
    flat_deim = deim_basis.reshape(cells * comps, deim_basis.shape[2])
    partial_g = lax.dot_general(
        flat_test, flat_deim, (((0,), (0,)), ((), ())), preferred_element_type=jnp.float32
    )
    offset = entering(counts, "rows", add_ints, jnp.zeros((1,), jnp.int32))
    slot_ids = jnp.arange(slots, dtype=jnp.int32)
    live = slot_ids < counts[0]
    row_ids = jnp.where(live, offset[0] + slot_ids, -1)
    first_cell = rank * cells
    widened = extended(trial_basis, (("rows", 0),), HALO)
    local = neighbours - (first_cell - HALO)
    picked = widened[local].astype(jnp.float32)
    contrib = jnp.einsum("snj,snjk->sk", jacobian, picked, precision=lax.Precision.HIGHEST)
    mode_ids = jnp.arange(total_modes, dtype=jnp.int32)[None, :]
    total_g = lax.psum(partial_g, "rows")
    folded = jnp.dot(
        total_g, sample_inverse, precision=lax.Precision.HIGHEST, preferred_element_type=jnp.float32
    )
    row_tags = jnp.broadcast_to(row_ids[:, None].astype(jnp.float32), (row_ids.shape[0], groups))
    arrived, arrived_tags = (
        lax.all_to_all(contrib, "rows", split_axis=1, concat_axis=0, tiled=True),
        lax.all_to_all(row_tags, "rows", split_axis=1, concat_axis=0, tiled=True),
    )
    received_ids = arrived_tags[:, 0].astype(jnp.int32)
    selector = (received_ids[:, None] == mode_ids).astype(jnp.float32)
    column_b = lax.dot_general(
        selector,
        arrived,
        (((0,), (0,)), ((), ())),
        precision=lax.Precision.HIGHEST,
        preferred_element_type=jnp.float32,
    )
    column_share = jnp.dot(
        folded, column_b, precision=lax.Precision.HIGHEST, preferred_element_type=jnp.float32
    )
    return lax.psum_scatter(column_share, "modes", scatter_dimension=0, tiled=True)


def solution(mesh):
    groups, parts = mesh.shape["rows"], mesh.shape["modes"]

    def shards(*args):
        cells, comps, width = args[2].shape
        modes = args[6].shape[0]
        slots = args[4].shape[0]
        tiled = (
            groups >= 3 and parts >= 2 and cells >= HALO
            and width % (8 * groups) == 0 and width % 128 == 0 and width % (16 * parts) == 0
            and modes % 128 == 0 and slots % 128 == 0 and cells % CHUNK == 0
        )
        return fused(groups, parts, *args) if tiled else plain(*args)

    in_specs = (
        P("rows", None, None),
        P("rows", None, "modes"),
        P("rows", None, None),
        P("rows", None, None),
        P("rows", None),
        P("rows"),
        P("modes", None),
    )
    out_specs = P("modes", "rows")
    return jax.shard_map(shards, mesh=mesh, in_specs=in_specs, out_specs=out_specs, check_vma=False)
```
